32 devices in a mesh: dp: 8 (over y, x, core), mp: 4 (over z).
Axes of the slice: x: 2, y: 2, z: 4, core: 2. Of those that a mesh axis runs over, the one named last changes fastest.
Arguments:
- block_input: bfloat16 [64, 256, 768], P(('dp', 'mp')), may hold values from -6 to 6
- lengths: int32 [64], P('dp'), may hold values from 16 to 256, as said below
- head_project: bfloat16 [3, 768, 768], P(None, None, 'mp'), may hold values from -0.21875 to 0.21875
- head_combine: bfloat16 [768, 768], P('mp'), may hold values from -0.875 to 0.875
- first_gain: float32 [768], replicated, may hold values from 0.5 to 1.5
- first_shift: float32 [768], replicated, may hold values from -4 to 4
- expand_weight: bfloat16 [768, 3072], P(None, 'mp'), may hold values from -0.21875 to 0.21875
- shrink_weight: bfloat16 [3072, 768], P('mp'), may hold values from -0.109375 to 0.109375
- adapter_down: bfloat16 [768, 768], replicated, may hold values from -0.21875 to 0.21875
- adapter_up: bfloat16 [16, 48, 768], replicated, may hold values from -0.875 to 0.875
- joining_query: bfloat16 [768, 768], replicated, may hold values from -0.21875 to 0.21875
- joining_key: bfloat16 [768, 768], replicated, may hold values from -0.875 to 0.875
- joining_value: bfloat16 [768, 768], replicated, may hold values from -0.21875 to 0.21875
- joining_bias: float32 [2, 768], replicated, may hold values from -4 to 4
- final_gain: float32 [768], replicated, may hold values from 0.5 to 1.5
- final_shift: float32 [768], replicated, may hold values from -4 to 4
- cotangent: bfloat16 [64, 256, 768], P(('dp', 'mp')), may hold values from -6 to 6
Outputs:
- block_output: bfloat16 [64, 256, 768], P(('dp', 'mp'))
- input_grad: float32 [64, 256, 768], P(('dp', 'mp'))
- joining_grad: float32 [3, 768, 768], replicated
- joining_bias_grad: float32 [2, 768], replicated
- final_gain_grad: float32 [768], replicated
- final_shift_grad: float32 [768], replicated
The draws below stay inside these ranges and needn't reach their ends.
Inputs may be any that keep to these rules, and one draw needn't show every extreme that they name: `lengths`: each sequence has 16 to 256 tokens, and some sequence has exactly 256.
All inputs are finite; a program needn't handle non-finite values.
Results may differ from the reference program's by a relative error of at most 0.03865.
Values may be sent and summed in bfloat16 or wider, within the bound.
No kernel may reach another device: no remote copies, remote signals or barrier semaphores. Data moves between devices by JAX's collectives and lax.ppermute only.
A program may use at most 128 MiB of HBM per device.

```python
import jax
import jax.numpy as jnp
from jax import lax

D = 768
HEAD_DIM = 64
FF = 3072
ADAPTERS = 16
BOTTLENECK = 48
LEN = 256
SEQ_DEV = 8
SEQS = 64


def draw_lengths(key, part):
    level_key, extra_key, pick_key = jax.random.split(key, 3)
    levels = jax.random.randint(level_key, (SEQS,), 0, 4)
    base_len = LEN // 16 * jnp.left_shift(jnp.ones((SEQS,), jnp.int32), levels.astype(jnp.int32))
    extra_len = jax.random.randint(extra_key, (SEQS,), 0, 1 << 20) % base_len
    chosen_index = jax.random.randint(pick_key, (), 0, SEQS)
    drawn = jnp.where(jnp.arange(SEQS) == chosen_index, LEN, base_len + extra_len)
    return drawn.astype(jnp.int32)


def level_of(rng, shape, pieces, least, largest):
    loudness, own = 1.0, jax.random.fold_in(rng, 6)
    for dim, parts in pieces:
        heights = jnp.exp(jax.random.uniform(jax.random.fold_in(own, dim), (parts,), jnp.float32, least / len(pieces), largest / len(pieces)))
        loudness = loudness * jnp.repeat(heights, shape[dim] // parts).reshape([-1 if axis == dim else 1 for axis in range(len(shape))])
    return loudness


def normal_values(rng, shape, spread, bound, cuts=(), kind=jnp.bfloat16):
    values = spread * jax.random.normal(rng, shape, jnp.float32)
    if cuts:
        values = values * level_of(rng, shape, cuts, -0.22, 0.18)
    return jnp.clip(values, -bound, bound).astype(kind)


def setup_inputs(seed: int = 0) -> dict:
    key_list = jax.random.split(jax.random.key(seed), 18)
    block_input = normal_values(key_list[0], (SEQS, LEN, D), 1.0, 6.0, ((0, 32),))
    lengths = draw_lengths(jax.random.fold_in(key_list[17], 71), 0)
    head_project = normal_values(key_list[2], (3, D, D), D ** -0.5, 0.21875, ((2, 4),))
    head_combine = normal_values(key_list[3], (D, D), (D // 16) ** -0.5, 0.875, ((0, 4),))
    first_gain = jnp.clip(1.0 + 0.1 * jax.random.normal(key_list[4], (D,), jnp.float32), 0.5, 1.5)
    first_shift = normal_values(key_list[5], (D,), 0.3, 4.0, (), jnp.float32)
    expand_weight = normal_values(key_list[6], (D, FF), D ** -0.5, 0.21875, ((1, 4),))
    shrink_weight = normal_values(key_list[7], (FF, D), FF ** -0.5, 0.109375, ((0, 4),))
    adapter_down = normal_values(key_list[8], (D, ADAPTERS * BOTTLENECK), D ** -0.5, 0.21875)
    adapter_up = normal_values(key_list[9], (ADAPTERS, BOTTLENECK, D), BOTTLENECK ** -0.5, 0.875)
    joining_query = normal_values(key_list[10], (D, D), D ** -0.5, 0.21875)
    joining_key = normal_values(key_list[11], (D, D), (D // 16) ** -0.5, 0.875)
    joining_value = normal_values(key_list[12], (D, D), D ** -0.5, 0.21875)
    joining_bias = normal_values(key_list[13], (2, D), 0.5, 4.0, (), jnp.float32)
    final_gain = jnp.clip(1.0 + 0.1 * jax.random.normal(key_list[14], (D,), jnp.float32), 0.5, 1.5)
    final_shift = normal_values(key_list[15], (D,), 0.3, 4.0, (), jnp.float32)
    cotangent = normal_values(key_list[16], (SEQS, LEN, D), 1.0, 6.0, ((0, 32),))
    return {"block_input": block_input, "lengths": lengths, "head_project": head_project, "head_combine": head_combine, "first_gain": first_gain, "first_shift": first_shift, "expand_weight": expand_weight, "shrink_weight": shrink_weight, "adapter_down": adapter_down, "adapter_up": adapter_up, "joining_query": joining_query, "joining_key": joining_key, "joining_value": joining_value, "joining_bias": joining_bias, "final_gain": final_gain, "final_shift": final_shift, "cotangent": cotangent}


@jax.custom_vjp
def low(v):
    return lax.optimization_barrier(v.astype(jnp.bfloat16)).astype(jnp.float32)

@jax.custom_vjp
def low_back(v):
    return v

def low_keep(v):
    return (low(v), None)

def low_pass(kept, grad):
    return (grad,)

def back_keep(v):
    return (v, None)

def back_low(kept, grad):
    return (low(grad),)
low.defvjp(low_keep, low_pass)
low_back.defvjp(back_keep, back_low)
highest = lax.Precision.HIGHEST

def layer_norm(value, gain, shift):
    centered = value - lax.optimization_barrier(jnp.mean(value, axis=-1, keepdims=True))
    inverse = lax.rsqrt(lax.optimization_barrier(jnp.mean(centered * centered, axis=-1, keepdims=True)) + 1e-12)
    return centered * inverse * gain + shift

def forward(block, group_lengths, frozen, query_weight, key_weight, value_weight, bias_pair, gain_two, shift_two):
    head_project, head_combine, first_gain, first_shift, expand_weight, shrink_weight, adapter_down, adapter_up = frozen
    seq_count = block.shape[0]
    head_count = D // HEAD_DIM
    tokens = seq_count * LEN
    flat = block.reshape(tokens, D)
    valid = jnp.arange(LEN)[None, :] < group_lengths[:, None]
    projected = low(low_back(jnp.einsum('td,kdc->ktc', flat, head_project, precision=highest)))
    projected = projected.reshape(3, seq_count, LEN, head_count, HEAD_DIM)
    logits = jnp.einsum('sqhe,skhe->shqk', projected[0], projected[1], precision=highest) * HEAD_DIM ** (-0.5)
    logits = low_back(jnp.where(valid[:, None, None, :], logits, -1000000000.0))
    probs_low = low(jax.nn.softmax(logits, axis=-1))
    heads_out = jnp.einsum('shqk,skhe->sqhe', probs_low, projected[2], precision=highest)
    heads_out = low(low_back(heads_out)).reshape(tokens, D)
    first_sum = flat + low_back(jnp.dot(heads_out, head_combine, precision=highest))
    normed_one = layer_norm(first_sum, first_gain, first_shift)
    up_value = low_back(jnp.dot(low(normed_one), expand_weight, precision=highest))
    activated_low = low(jax.nn.gelu(up_value, approximate=False))
    branch = low_back(jnp.dot(activated_low, shrink_weight, precision=highest))
    branch_low = low(branch)
    down_value = low_back(jnp.dot(branch_low, adapter_down, precision=highest))
    hidden_low = low(jax.nn.relu(down_value)).reshape(tokens, ADAPTERS, BOTTLENECK)
    adapted = branch[:, None, :] + jnp.einsum('nab,abd->nad', hidden_low, adapter_up, precision=highest)
    adapted_low = low(low_back(adapted))
    query_low = low(low_back(jnp.dot(branch_low, query_weight, precision=highest) + bias_pair[0]))
    probe_low = low(low_back(jnp.dot(query_low, key_weight.T, precision=highest)))
    scores = jnp.einsum('nad,nd->na', adapted_low, probe_low, precision=highest) * D ** (-0.5)
    chosen_low = low(jax.nn.softmax(low_back(scores), axis=-1))
    blend_low = low(low_back(jnp.einsum('na,nad->nd', chosen_low, adapted_low, precision=highest)))
    second_sum = low_back(jnp.dot(blend_low, value_weight, precision=highest)) + bias_pair[1] + normed_one
    output = layer_norm(second_sum, gain_two, shift_two)
    return (output * valid.reshape(tokens, 1)).reshape(seq_count, LEN, D)

def reference(block_input, lengths, head_project, head_combine, first_gain, first_shift, expand_weight, shrink_weight, adapter_down, adapter_up, joining_query, joining_key, joining_value, joining_bias, final_gain, final_shift, cotangent):
    groups = block_input.shape[0] // SEQ_DEV
    frozen = tuple((array.astype(jnp.float32) for array in (head_project, head_combine, first_gain, first_shift, expand_weight, shrink_weight, adapter_down, adapter_up)))
    trained = tuple((array.astype(jnp.float32) for array in (joining_query, joining_key, joining_value, joining_bias, final_gain, final_shift)))
    inputs_grouped = block_input.astype(jnp.float32).reshape(groups, SEQ_DEV, LEN, D)
    lengths_grouped = lengths.reshape(groups, SEQ_DEV)
    grads_grouped = cotangent.astype(jnp.float32).reshape(groups, SEQ_DEV, LEN, D)

    def one_group(totals, entry):
        group_input, group_lengths, group_cotangent = entry

        def run(block, query_weight, key_weight, value_weight, bias_pair, gain_two, shift_two):
            return forward(block, group_lengths, frozen, query_weight, key_weight, value_weight, bias_pair, gain_two, shift_two)
        output, pull_back = jax.vjp(run, group_input, *trained)
        grads = pull_back(group_cotangent)
        totals = tuple((total + grad for total, grad in zip(totals, grads[1:])))
        return (totals, (output.astype(jnp.bfloat16), grads[0]))
    start_totals = tuple((jnp.zeros_like(array) for array in trained))
    totals, (outputs, input_grads) = lax.scan(one_group, start_totals, (inputs_grouped, lengths_grouped, grads_grouped))
    joining_grad = jnp.stack([totals[0], totals[1], totals[2]])
    return (outputs.reshape(block_input.shape), input_grads.reshape(block_input.shape), joining_grad, totals[3], totals[4], totals[5])
```

```python
import jax
import jax.numpy as jnp
from jax import lax
from jax.sharding import PartitionSpec as P

HEAD_DIM = 64
EPS = 1e-12
BF = jnp.bfloat16
F32 = jnp.float32


def dot(a, b):
    return jnp.dot(a, b, preferred_element_type=F32)


def dot_t(a, b):
    return lax.dot_general(a, b, (((1,), (1,)), ((), ())), preferred_element_type=F32)


def dot_tt(a, b):
    return lax.dot_general(a, b, (((0,), (0,)), ((), ())), preferred_element_type=F32)


def normalize(value, gain, shift):
    centered = value - jnp.mean(value, axis=-1, keepdims=True)
    inverse = lax.rsqrt(jnp.mean(centered * centered, axis=-1, keepdims=True) + EPS)
    normed = centered * inverse
    return (normed * gain + shift, normed, inverse)


def normalize_back(grad, normed, inverse, gain):
    scaled = grad * gain
    return inverse * (
        scaled
        - jnp.mean(scaled, axis=-1, keepdims=True)
        - normed * jnp.mean(scaled * normed, axis=-1, keepdims=True)
    )


class Links:
    def __init__(self):
        self.dp = lax.axis_size("dp")
        self.mp = lax.axis_size("mp")
        index = lax.axis_index("dp")
        self.low = index % 2
        mid = (index // 2) % 2
        high = (index // 4) % 2
        self.first = jnp.where(self.low == 0, mid, high)
        self.second = jnp.where(self.low == 0, high, mid)
        self.piece = self.low * 4 + self.second * 2 + self.first
        self.first_perm = [(i, i ^ (2 if i % 2 == 0 else 4)) for i in range(self.dp)]
        self.second_perm = [(i, i ^ (4 if i % 2 == 0 else 2)) for i in range(self.dp)]
        self.low_perm = [(i, i ^ 1) for i in range(self.dp)]

    def shift(self, value, step):
        return lax.ppermute(value, "mp", [(i, (i + step) % self.mp) for i in range(self.mp)])

    def join(self, value, perm, bit):
        other = lax.ppermute(value, "dp", perm)
        return jnp.where(
            bit == 0, jnp.concatenate([value, other], 1), jnp.concatenate([other, value], 1)
        )

    def gather(self, shard):
        rows = shard.shape[0] // 8
        piece = lax.dynamic_slice_in_dim(shard, self.piece * rows, rows)
        stacked = jnp.stack([self.shift(piece, step) for step in range(1, self.mp)])
        stacked = self.join(stacked, self.first_perm, self.first)
        stacked = self.join(stacked, self.second_perm, self.second)
        stacked = self.join(stacked, self.low_perm, self.low)
        return [shard] + [stacked[k] for k in range(self.mp - 1)]

    def halve(self, value, axis, perm, bit):
        rows = value.shape[0] // 2
        keep = lax.dynamic_slice_in_dim(value, bit * rows, rows)
        send = lax.dynamic_slice_in_dim(value, (1 - bit) * rows, rows)
        return keep + lax.ppermute(send.astype(BF), axis, perm).astype(F32)

    def total(self, value):
        mp_index = lax.axis_index("mp")
        steps = [
            ("dp", self.low_perm, self.low),
            ("dp", self.first_perm, self.first),
            ("dp", self.second_perm, self.second),
        ]
        bit = 1
        while bit < self.mp:
            steps.append(("mp", [(i, i ^ bit) for i in range(self.mp)], (mp_index // bit) % 2))
            bit *= 2
        for axis, perm, own in steps:
            value = self.halve(value, axis, perm, own)
        if self.dp > 8:
            groups = [[j * 8 + i for j in range(self.dp // 8)] for i in range(8)]
            value = lax.psum(value, "dp", axis_index_groups=groups)
        value = value.astype(BF)
        for axis, perm, own in reversed(steps):
            other = lax.ppermute(value, axis, perm)
            value = jnp.where(
                own == 0, jnp.concatenate([value, other]), jnp.concatenate([other, value])
            )
        return value.astype(F32)

    def total_small(self, value):
        for bit in range((self.dp - 1).bit_length()):
            value = value + lax.ppermute(value, "dp", [(i, i ^ (1 << bit)) for i in range(self.dp)])
        for bit in range((self.mp - 1).bit_length()):
            value = value + lax.ppermute(value, "mp", [(i, i ^ (1 << bit)) for i in range(self.mp)])
        return value


def local(
    block_input,
    lengths,
    head_project,
    head_combine,
    first_gain,
    first_shift,
    expand_weight,
    shrink_weight,
    adapter_down,
    adapter_up,
    joining_query,
    joining_key,
    joining_value,
    joining_bias,
    final_gain,
    final_shift,
    cotangent,
):
    own_count, full_len, width = block_input.shape
    tokens = own_count * full_len
    columns = head_project.shape[2]
    heads = columns // HEAD_DIM
    adapters, bottleneck = adapter_up.shape[:2]
    inner = adapters * bottleneck
    head_scale = HEAD_DIM ** (-0.5)
    joining_scale = width ** (-0.5)
    links = Links()

    offset = lax.axis_index("mp") * own_count
    own_lengths = lax.dynamic_slice_in_dim(lengths, offset, own_count)
    valid = jnp.arange(full_len)[None, :] < own_lengths[:, None]
    row_mask = valid.reshape(tokens, 1).astype(F32)

    projects = links.gather(head_project.reshape(3 * width, columns))
    combines = links.gather(head_combine)
    expands = links.gather(expand_weight)
    shrinks = links.gather(shrink_weight)

    flat = block_input.reshape(tokens, width)
    saved = []
    attended = 0.0
    for project, combine in zip(projects, combines):
        project = project.reshape(3, width, columns)
        projected = jnp.einsum("td,kdc->ktc", flat, project, preferred_element_type=F32).astype(BF)
        projected = projected.reshape(3, own_count, full_len, heads, HEAD_DIM)
        queries, keys, values = projected[0], projected[1], projected[2]
        logits = (
            jnp.einsum("sqhe,skhe->shqk", queries, keys, preferred_element_type=F32) * head_scale
        )
        logits = jnp.where(valid[:, None, None, :], logits, -1000000000.0)
        top = jnp.max(logits, axis=-1, keepdims=True)
        raised = jnp.exp(logits - top)
        probs = raised / jnp.sum(raised, axis=-1, keepdims=True)
        out = jnp.einsum("shqk,skhe->sqhe", probs.astype(BF), values, preferred_element_type=F32)
        attended = attended + dot(out.reshape(tokens, columns).astype(BF), combine)
        saved.append((project, combine, queries, keys, values, probs))

    first_sum = flat.astype(F32) + attended
    normed_one, hat_one, inv_one = normalize(first_sum, first_gain, first_shift)
    normed_low = normed_one.astype(BF)
    branch = 0.0
    slopes = []
    for expand, shrink in zip(expands, shrinks):
        up_value = dot(normed_low, expand)
        cdf = 0.5 * (1.0 + lax.erf(up_value * (0.5**0.5)))
        slope = cdf + up_value * jnp.exp(-0.5 * up_value * up_value) * (0.3989422804014327)
        branch = branch + dot((up_value * cdf).astype(BF), shrink)
        slopes.append(slope)

    up_matrix = adapter_up.reshape(inner, width)
    member = (
        jnp.arange(inner)[:, None] // bottleneck == jnp.arange(adapters)[None, :]
    ).astype(BF)

    def per_adapter(value):
        high = value.astype(BF)
        return dot(high, member) + dot((value - high.astype(F32)).astype(BF), member)

    def spread(value):
        return dot_t(value, member)

    branch_low = branch.astype(BF)
    down_value = dot(branch_low, adapter_down)
    hidden = jnp.maximum(down_value, 0.0).astype(BF).astype(F32)
    query_low = (dot(branch_low, joining_query) + joining_bias[0]).astype(BF)
    probe_low = dot_t(query_low, joining_key).astype(BF)
    probe = probe_low.astype(F32)
    probe_up = dot_t(probe_low, up_matrix)
    scores = joining_scale * (
        jnp.sum(branch * probe, axis=-1, keepdims=True) + per_adapter(hidden * probe_up)
    )
    chosen = jax.nn.softmax(scores, axis=-1)
    chosen_low = chosen.astype(BF)
    chosen_sum = jnp.sum(chosen_low.astype(F32), axis=-1, keepdims=True)
    chosen_wide = spread(chosen_low)
    blend_low = (
        branch * chosen_sum + dot((chosen_wide * hidden).astype(BF), up_matrix)
    ).astype(BF)
    second_sum = dot(blend_low, joining_value) + joining_bias[1] + normed_one
    output, hat_two, inv_two = normalize(second_sum, final_gain, final_shift)
    block_output = (output * row_mask).reshape(own_count, full_len, width).astype(BF)

    grad_out = cotangent.astype(F32).reshape(tokens, width) * row_mask
    gain_grad = jnp.sum(grad_out * hat_two, axis=0)
    shift_grad = jnp.sum(grad_out, axis=0)
    second_grad = normalize_back(grad_out, hat_two, inv_two, final_gain)
    value_bias_grad = jnp.sum(second_grad, axis=0)
    second_low = second_grad.astype(BF)
    value_weight_grad = links.total(dot_tt(blend_low, second_low))
    blend_grad_low = dot_t(second_low, joining_value).astype(BF)
    blend_grad = blend_grad_low.astype(F32)
    blend_up = dot_t(blend_grad_low, up_matrix)
    weight_grad = jnp.sum(branch * blend_grad, axis=-1, keepdims=True) + per_adapter(
        hidden * blend_up
    )
    score_grad_low = (
        chosen * (weight_grad - jnp.sum(chosen * weight_grad, axis=-1, keepdims=True))
    ).astype(BF)
    score_sum = jnp.sum(score_grad_low.astype(F32), axis=-1, keepdims=True)
    score_wide = spread(score_grad_low)
    probe_grad_low = (
        joining_scale * (branch * score_sum + dot((score_wide * hidden).astype(BF), up_matrix))
    ).astype(BF)
    key_weight_grad = links.total(dot_tt(probe_grad_low, query_low))
    query_grad_low = dot(probe_grad_low, joining_key).astype(BF)
    query_bias_grad = jnp.sum(query_grad_low, axis=0, dtype=F32)
    query_weight_grad = links.total(dot_tt(branch_low, query_grad_low))
    small = links.total_small(jnp.stack([query_bias_grad, value_bias_grad, gain_grad, shift_grad]))
    down_grad_low = jnp.where(
        down_value > 0, chosen_wide * blend_up + joining_scale * score_wide * probe_up, 0.0
    ).astype(BF)
    branch_grad_low = (
        chosen_sum * blend_grad
        + joining_scale * score_sum * probe
        + dot_t(down_grad_low, adapter_down)
        + dot_t(query_grad_low, joining_query)
    ).astype(BF)

    normed_grad = second_grad
    for expand, shrink, slope in zip(expands, shrinks, slopes):
        up_grad_low = (dot_t(branch_grad_low, shrink) * slope).astype(BF)
        normed_grad = normed_grad + dot_t(up_grad_low, expand)
    first_grad = normalize_back(normed_grad, hat_one, inv_one, first_gain)
    first_low = first_grad.astype(BF)
    input_grad = first_grad
    for project, combine, queries, keys, values, probs in saved:
        heads_grad = dot_t(first_low, combine).astype(BF)
        heads_grad = heads_grad.reshape(own_count, full_len, heads, HEAD_DIM)
        probs_grad = jnp.einsum("sqhe,skhe->shqk", heads_grad, values, preferred_element_type=F32)
        value_part = jnp.einsum(
            "shqk,sqhe->skhe", probs.astype(BF), heads_grad, preferred_element_type=F32
        )
        delta = jnp.sum(probs_grad * probs, axis=-1, keepdims=True)
        logits_grad = (probs * (probs_grad - delta)).astype(BF)
        query_part = head_scale * jnp.einsum(
            "shqk,skhe->sqhe", logits_grad, keys, preferred_element_type=F32
        )
        key_part = head_scale * jnp.einsum(
            "shqk,sqhe->skhe", logits_grad, queries, preferred_element_type=F32
        )
        parts = jnp.stack([query_part, key_part, value_part]).astype(BF)
        input_grad = input_grad + jnp.einsum(
            "ktc,kdc->td",
            parts.reshape(3, tokens, columns),
            project,
            preferred_element_type=F32,
        )
    return (
        block_output,
        input_grad.reshape(own_count, full_len, width),
        jnp.stack([query_weight_grad, key_weight_grad, value_weight_grad]),
        small[:2],
        small[2],
        small[3],
    )


def solution(mesh):
    return jax.shard_map(
        local,
        mesh=mesh,
        in_specs=(
            P(("dp", "mp"), None, None),
            P("dp"),
            P(None, None, "mp"),
            P("mp", None),
            P(),
            P(),
            P(None, "mp"),
            P("mp", None),
            P(),
            P(),
            P(),
            P(),
            P(),
            P(),
            P(),
            P(),
            P(("dp", "mp"), None, None),
        ),
        out_specs=(P(("dp", "mp"), None, None), P(("dp", "mp"), None, None), P(), P(), P(), P()),
        check_vma=False,
    )
```

```python
import functools

import jax
import jax.numpy as jnp
from jax import lax
from jax.experimental import pallas as pl
from jax.experimental.pallas import tpu as pltpu
from jax.sharding import PartitionSpec as P

HEAD_DIM = 64
EPS = 1e-12
BF = jnp.bfloat16
F32 = jnp.float32
LANES = 128
STRIDE = 256
SLICE = 256
CHUNK = 32


def dot(a, b):
    return jnp.dot(a, b, preferred_element_type=F32)


def dot_t(a, b):
    return lax.dot_general(a, b, (((1,), (1,)), ((), ())), preferred_element_type=F32)


def dot_tt(a, b):
    return lax.dot_general(a, b, (((0,), (0,)), ((), ())), preferred_element_type=F32)


def hat_of(value):
    centered = value - jnp.mean(value, axis=-1, keepdims=True)
    inverse = lax.rsqrt(jnp.mean(centered * centered, axis=-1, keepdims=True) + EPS)
    return centered * inverse, inverse


def normalize_back(grad, normed, inverse, gain):
    scaled = grad * gain
    return inverse * (
        scaled
        - jnp.mean(scaled, axis=-1, keepdims=True)
        - normed * jnp.mean(scaled * normed, axis=-1, keepdims=True)
    )


def by_rows(count, body):
    @pl.loop(0, count // CHUNK)
    def _(i):
        body(pl.ds(pl.multiple_of(i * CHUNK, CHUNK), CHUNK))


class Links:
    def __init__(self):
        self.dp = lax.axis_size("dp")
        self.mp = lax.axis_size("mp")
        index = lax.axis_index("dp")
        self.low = index % 2
        mid = (index // 2) % 2
        high = (index // 4) % 2
        self.first = jnp.where(self.low == 0, mid, high)
        self.second = jnp.where(self.low == 0, high, mid)
        self.piece = self.low * 4 + self.second * 2 + self.first
        self.first_perm = [(i, i ^ (2 if i % 2 == 0 else 4)) for i in range(self.dp)]
        self.second_perm = [(i, i ^ (4 if i % 2 == 0 else 2)) for i in range(self.dp)]
        self.low_perm = [(i, i ^ 1) for i in range(self.dp)]
        self.mp_index = lax.axis_index("mp")
        self.mp_bits = []
        bit = 1
        while bit < self.mp:
            self.mp_bits.append(([(i, i ^ bit) for i in range(self.mp)], (self.mp_index // bit) % 2))
            bit *= 2

    def offsets(self, rows):
        mine = [
            self.low * 4 + (self.second ^ (j // 2)) * 2 + (self.first ^ (j % 2)) for j in range(4)
        ]
        theirs = [
            (1 - self.low) * 4 + (self.first ^ (j // 2)) * 2 + (self.second ^ (j % 2))
            for j in range(4)
        ]
        return jnp.stack(mine + theirs).astype(jnp.int32) * rows

    def gather(self, shard):
        rows = shard.shape[0] // 8
        held = lax.dynamic_slice_in_dim(shard, self.piece * rows, rows)[None]
        for perm, _ in self.mp_bits:
            held = jnp.concatenate([held, lax.ppermute(held, "mp", perm)])
        held = held[1:][None]
        held = jnp.concatenate([held, lax.ppermute(held, "dp", self.first_perm)])
        held = jnp.concatenate([held, lax.ppermute(held, "dp", self.second_perm)])
        return held, lax.ppermute(held, "dp", self.low_perm)

    def total(self, value, small):
        steps = [
            ("dp", self.low_perm, self.low),
            ("dp", self.first_perm, self.first),
            ("dp", self.second_perm, self.second),
        ] + [("mp", perm, own) for perm, own in self.mp_bits]
        for axis, perm, own in steps:
            rows = value.shape[1] // 2
            keep = lax.dynamic_slice_in_dim(value, own * rows, rows, 1)
            send = lax.dynamic_slice_in_dim(value, (1 - own) * rows, rows, 1).astype(BF)
            high = small.astype(BF)
            rest = (small - high.astype(F32)).astype(BF)
            flat = send.reshape(-1, send.shape[2])
            got = lax.ppermute(jnp.concatenate([flat, high, rest]), axis, perm).astype(F32)
            value = keep + got[: flat.shape[0]].reshape(keep.shape)
            small = high.astype(F32) + rest.astype(F32)
            small = small + got[-8:-4] + got[-4:]
        if self.dp > 8:
            groups = [[j * 8 + i for j in range(self.dp // 8)] for i in range(8)]
            value, small = lax.psum((value, small), "dp", axis_index_groups=groups)
        value = value.astype(BF)
        for axis, perm, own in reversed(steps):
            other = lax.ppermute(value, axis, perm)
            value = jnp.where(
                own == 0, jnp.concatenate([value, other], 1), jnp.concatenate([other, value], 1)
            )
        return value.astype(F32), small


def fetch(target, mine, theirs, offsets, other, sem):
    rows = mine.shape[2]
    copies = []
    for j in range(4):
        for half, source in enumerate((mine, theirs)):
            at = pl.multiple_of(offsets[half * 4 + j], 16)
            copies.append(
                pltpu.make_async_copy(
                    source.at[j, other], target.at[pl.ds(at, rows)], sem.at[half * 4 + j]
                )
            )
    for copy in copies:
        copy.start()
    return copies


def head_list(columns):
    heads = []
    for head in range(columns // HEAD_DIM):
        base = head * HEAD_DIM // LANES * LANES
        wide = min(LANES, columns - base)
        heads.append((base, wide, (head * HEAD_DIM - base) // HEAD_DIM if wide == LANES else None))
    return heads


def own_lanes(wide, half, kind):
    lane = lax.broadcasted_iota(jnp.int32, (1, wide), 1)
    return jnp.where(lane // HEAD_DIM == half, 1.0, 0.0).astype(kind)


def put_head(ref, rows, base, wide, half, value):
    if half is None:
        ref[rows, base : base + wide] = value.astype(ref.dtype)
    elif half == 0:
        ref[rows, base : base + wide] = value.astype(ref.dtype)
    else:
        lane = lax.broadcasted_iota(jnp.int32, value.shape, 1)
        kept = ref[rows, base : base + wide].astype(F32)
        ref[rows, base : base + wide] = jnp.where(lane // HEAD_DIM == half, value, kept).astype(
            ref.dtype
        )


def head_probs(qkv, rows, base, wide, half, length):
    queries = qkv[rows, base : base + wide]
    if half is not None:
        queries = queries * own_lanes(wide, half, BF)
    keys = qkv[rows, STRIDE + base : STRIDE + base + wide]
    logits = dot_t(queries, keys) * HEAD_DIM ** (-0.5)
    place = lax.broadcasted_iota(jnp.int32, logits.shape, 1)
    logits = jnp.where(place < length, logits, -1000000000.0)
    raised = jnp.exp(logits - jnp.max(logits, axis=-1, keepdims=True))
    return raised / jnp.sum(raised, axis=-1, keepdims=True)


def attend(x, weights, qkv, heads_out, lengths, columns, count, full_len):
    for part in range(3):
        qkv[:, part * STRIDE : part * STRIDE + columns] = dot_t(
            x[...], weights[part * columns : (part + 1) * columns, :]
        ).astype(BF)
    for s in range(count):
        rows = slice(s * full_len, (s + 1) * full_len)
        for base, wide, half in head_list(columns):
            probs = head_probs(qkv, rows, base, wide, half, lengths[s]).astype(BF)
            values = qkv[rows, 2 * STRIDE + base : 2 * STRIDE + base + wide]
            put_head(heads_out, rows, base, wide, half, dot(probs, values))


def attend_own_kernel(lengths, x, weights, attended, qkv, heads_out, *, columns, full_len):
    count = x.shape[0] // full_len
    attend(x, weights, qkv, heads_out, lengths, columns, count, full_len)
    attended[...] = dot(heads_out[...], weights[3 * columns :, :])


def attend_rest_kernel(
    lengths, offsets, x, attended, gain, shift, mine, theirs,
    first_sum, normed_low, qkv, weights, heads_out, sem, *, columns, full_len,
):
    others = mine.shape[1]
    count = x.shape[0] // full_len
    copies = [
        fetch(weights.at[r], mine, theirs, offsets, r, sem.at[r]) for r in range(others)
    ]
    first_sum[...] = x[...].astype(F32) + attended[...]
    for r in range(others):
        for copy in copies[r]:
            copy.wait()
        attend(x, weights.at[r], qkv.at[r], heads_out, lengths, columns, count, full_len)
        first_sum[...] += dot(heads_out[...], weights[r, 3 * columns :, :])

    def norm(rows):
        hat, _ = hat_of(first_sum[rows, :])
        normed_low[rows, :] = (hat * gain[...] + shift[...]).astype(BF)

    by_rows(x.shape[0], norm)


def feed(normed, expand, shrink, slopes, branch, start):
    units = expand.shape[1]
    for base in range(0, units, SLICE):
        up_value = dot(normed[...], expand[:, base : base + SLICE])
        cdf = 0.5 + 0.5 * lax.erf(up_value * (0.5**0.5))
        slope = cdf + up_value * (jnp.exp(-0.5 * up_value * up_value) * 0.3989422804014327)
        slopes[:, base : base + SLICE] = slope.astype(BF)
        term = dot((up_value * cdf).astype(BF), shrink[base : base + SLICE, :])
        if start and base == 0:
            branch[...] = term
        else:
            branch[...] += term


def feed_own_kernel(normed, expand, shrink, branch, slopes):
    feed(normed, expand, shrink, slopes, branch, True)


def feed_rest_kernel(
    offsets, normed, partial, expand_mine, expand_theirs, shrink_mine, shrink_theirs,
    branch, slopes, expand, shrink, sem,
):
    others = expand_mine.shape[1]
    copies = [
        fetch(expand.at[r], expand_mine, expand_theirs, offsets, r, sem.at[0, r])
        + fetch(shrink.at[r], shrink_mine, shrink_theirs, offsets, r, sem.at[1, r])
        for r in range(others)
    ]
    branch[...] = partial[...]
    for r in range(others):
        for copy in copies[r]:
            copy.wait()
        feed(normed, expand.at[r], shrink.at[r], slopes.at[r], branch, False)


def adapters_kernel(
    lengths, branch_ref, first_sum, cotangent, first_gain, first_shift, down, up_matrix, query_w,
    key_w, value_w, bias, final_gain, final_shift, member,
    block_output, second_grad_ref, branch_grad_ref, weight_grads, small,
    *, adapters, scale,
):
    step = pl.program_id(0)
    rows = branch_ref.shape[0]
    valid = lax.broadcasted_iota(jnp.int32, (rows, 1), 0) < lengths[step]
    row_mask = jnp.where(valid, 1.0, 0.0)
    real = lax.broadcasted_iota(jnp.int32, (1, LANES), 1) < adapters

    def per_adapter(value):
        high = value.astype(BF)
        rest = (value - high.astype(F32)).astype(BF)
        return dot(high, member[...]) + dot(rest, member[...])

    def spread(value):
        return dot_t(value, member[...])

    def gather_grad(k, left, right):
        part = dot_tt(left, right)

        @pl.when(step == 0)
        def _():
            weight_grads[k] = part

        @pl.when(step > 0)
        def _():
            weight_grads[k] += part

    branch = branch_ref[...]
    branch_low = branch.astype(BF)
    down_value = dot(branch_low, down[...])
    hidden = jnp.maximum(down_value, 0.0).astype(BF).astype(F32)
    query_low = (dot(branch_low, query_w[...]) + bias[0:1, :]).astype(BF)
    probe_low = dot_t(query_low, key_w[...]).astype(BF)
    probe = probe_low.astype(F32)
    probe_up = dot_t(probe_low, up_matrix[...])
    scores = scale * (
        jnp.sum(branch * probe, axis=-1, keepdims=True) + per_adapter(hidden * probe_up)
    )
    scores = jnp.where(real, scores, -3.0e38)
    raised = jnp.exp(scores - jnp.max(scores, axis=-1, keepdims=True))
    chosen = raised / jnp.sum(raised, axis=-1, keepdims=True)
    chosen_low = chosen.astype(BF)
    chosen_sum = jnp.sum(chosen_low.astype(F32), axis=-1, keepdims=True)
    chosen_wide = spread(chosen_low)
    blend_low = (
        branch * chosen_sum + dot((chosen_wide * hidden).astype(BF), up_matrix[...])
    ).astype(BF)
    hat_one, _ = hat_of(first_sum[...])
    normed_one = hat_one * first_gain[...] + first_shift[...]
    second_sum = dot(blend_low, value_w[...]) + bias[1:2, :] + normed_one
    hat_two, inv_two = hat_of(second_sum)
    block_output[...] = ((hat_two * final_gain[...] + final_shift[...]) * row_mask).astype(BF)

    grad_out = cotangent[...].astype(F32) * row_mask
    gain_grad = jnp.sum(grad_out * hat_two, axis=0, keepdims=True)
    shift_grad = jnp.sum(grad_out, axis=0, keepdims=True)
    second_grad = normalize_back(grad_out, hat_two, inv_two, final_gain[...])
    second_grad_ref[...] = second_grad
    value_bias_grad = jnp.sum(second_grad, axis=0, keepdims=True)
    second_low = second_grad.astype(BF)
    gather_grad(2, blend_low, second_low)
    blend_grad_low = dot_t(second_low, value_w[...]).astype(BF)
    blend_grad = blend_grad_low.astype(F32)
    blend_up = dot_t(blend_grad_low, up_matrix[...])
    weight_grad = jnp.sum(branch * blend_grad, axis=-1, keepdims=True) + per_adapter(
        hidden * blend_up
    )
    weight_grad = jnp.where(real, weight_grad, 0.0)
    score_grad_low = (
        chosen * (weight_grad - jnp.sum(chosen * weight_grad, axis=-1, keepdims=True))
    ).astype(BF)
    score_sum = jnp.sum(score_grad_low.astype(F32), axis=-1, keepdims=True)
    score_wide = spread(score_grad_low)
    probe_grad_low = (
        scale * (branch * score_sum + dot((score_wide * hidden).astype(BF), up_matrix[...]))
    ).astype(BF)
    gather_grad(1, probe_grad_low, query_low)
    query_grad_low = dot(probe_grad_low, key_w[...]).astype(BF)
    gather_grad(0, branch_low, query_grad_low)
    query_bias_grad = jnp.sum(query_grad_low.astype(F32), axis=0, keepdims=True)
    down_grad_low = jnp.where(
        down_value > 0, chosen_wide * blend_up + scale * score_wide * probe_up, 0.0
    ).astype(BF)
    branch_grad_ref[...] = (
        chosen_sum * blend_grad
        + scale * score_sum * probe
        + dot_t(down_grad_low, down[...])
        + dot_t(query_grad_low, query_w[...])
    ).astype(BF)
    for k, part in enumerate((query_bias_grad, value_bias_grad, gain_grad, shift_grad)):

        @pl.when(step == 0)
        def _(k=k, part=part):
            small[k : k + 1, :] = part

        @pl.when(step > 0)
        def _(k=k, part=part):
            small[k : k + 1, :] += part


def feed_back(branch_grad, expand, shrink, slopes, normed_grad):
    for base in range(0, expand.shape[1], SLICE):
        up_grad = dot_t(branch_grad[...], shrink[base : base + SLICE, :])
        up_grad = (up_grad * slopes[:, base : base + SLICE].astype(F32)).astype(BF)
        normed_grad[...] += dot_t(up_grad, expand[:, base : base + SLICE])


def feed_own_back_kernel(branch_grad, slopes, second_grad, expand, shrink, normed_grad):
    normed_grad[...] = second_grad[...]
    feed_back(branch_grad, expand, shrink, slopes, normed_grad)


def feed_rest_back_kernel(
    offsets, branch_grad, slopes, partial, first_sum, gain,
    expand_mine, expand_theirs, shrink_mine, shrink_theirs,
    first_grad, first_low, expand, shrink, sem,
):
    others = expand_mine.shape[1]
    copies = [
        fetch(expand.at[r], expand_mine, expand_theirs, offsets, r, sem.at[0, r])
        + fetch(shrink.at[r], shrink_mine, shrink_theirs, offsets, r, sem.at[1, r])
        for r in range(others)
    ]
    first_grad[...] = partial[...]
    for r in range(others):
        for copy in copies[r]:
            copy.wait()
        feed_back(branch_grad, expand.at[r], shrink.at[r], slopes.at[r], first_grad)

    def norm(rows):
        hat, inverse = hat_of(first_sum[rows, :])
        grad = normalize_back(first_grad[rows, :], hat, inverse, gain[...])
        first_grad[rows, :] = grad
        first_low[rows, :] = grad.astype(BF)

    by_rows(branch_grad.shape[0], norm)


def attend_back(first_low, weights, qkv, grads, heads_grad, lengths, columns, count, full_len):
    heads_grad[...] = dot_t(first_low[...], weights[3 * columns :, :]).astype(BF)
    scale = HEAD_DIM ** (-0.5)
    for s in range(count):
        rows = slice(s * full_len, (s + 1) * full_len)
        for base, wide, half in head_list(columns):
            probs = head_probs(qkv, rows, base, wide, half, lengths[s])
            grad = heads_grad[rows, base : base + wide]
            own = grad if half is None else grad * own_lanes(wide, half, BF)
            values = qkv[rows, 2 * STRIDE + base : 2 * STRIDE + base + wide]
            probs_grad = dot_t(own, values)
            delta = jnp.sum(probs_grad * probs, axis=-1, keepdims=True)
            logits_grad = (probs * (probs_grad - delta)).astype(BF)
            keys = qkv[rows, STRIDE + base : STRIDE + base + wide]
            queries = qkv[rows, base : base + wide]
            put_head(grads.at[0], rows, base, wide, half, dot(logits_grad, keys) * scale)
            put_head(grads.at[1], rows, base, wide, half, dot_tt(logits_grad, queries) * scale)
            put_head(grads.at[2], rows, base, wide, half, dot_tt(probs.astype(BF), grad))


def project_back(grads, weights, input_grad, columns):
    for part in range(3):
        input_grad[...] += dot(
            grads[part], weights[part * columns : (part + 1) * columns, :]
        )


def attend_own_back_kernel(
    lengths, first_low, qkv, weights, first_grad, input_grad, grads, heads_grad,
    *, columns, full_len,
):
    count = first_low.shape[0] // full_len
    input_grad[...] = first_grad[...]
    attend_back(first_low, weights, qkv, grads, heads_grad, lengths, columns, count, full_len)
    project_back(grads, weights, input_grad, columns)


def attend_rest_back_kernel(
    lengths, offsets, first_low, qkv, partial, mine, theirs,
    input_grad, weights, grads, heads_grad, sem, *, columns, full_len, others,
):
    count = first_low.shape[0] // full_len
    copies = [
        fetch(weights.at[k], mine, theirs, offsets, r, sem.at[k]) for k, r in enumerate(others)
    ]
    input_grad[...] = partial[...]
    for k, r in enumerate(others):
        for copy in copies[k]:
            copy.wait()
        attend_back(
            first_low, weights.at[k], qkv.at[k], grads, heads_grad, lengths, columns, count, full_len
        )
        project_back(grads, weights.at[k], input_grad, columns)


SMEM = pl.BlockSpec(memory_space=pltpu.SMEM)
VMEM = pl.BlockSpec(memory_space=pltpu.VMEM)
HBM = pl.BlockSpec(memory_space=pl.ANY)


def call(kernel, specs, outs, scratch=(), name=None, **static):
    return pl.pallas_call(
        functools.partial(kernel, **static) if static else kernel,
        in_specs=list(specs),
        out_specs=tuple(VMEM for _ in outs),
        out_shape=tuple(outs),
        scratch_shapes=list(scratch),
        name=name,
    )


def layer(
    lengths, block, cotangent, heads_own, expand_own, shrink_own, heads_rest, expand_rest,
    shrink_rest, offsets, first_gain, first_shift, adapter_down, adapter_up, joining_query,
    joining_key, joining_value, joining_bias, final_gain, final_shift, columns, full_len,
):
    tokens, width = block.shape
    count = tokens // full_len
    others = heads_rest[0].shape[1]
    shard_rows = heads_own.shape[0]
    units = expand_own.shape[1]
    adapters, bottleneck = adapter_up.shape[:2]
    inner = adapters * bottleneck
    wide = jax.ShapeDtypeStruct((tokens, width), F32)
    low = jax.ShapeDtypeStruct((tokens, width), BF)
    saved = (tokens, 3 * STRIDE)
    dims = dict(columns=columns, full_len=full_len)
    dma = pltpu.SemaphoreType.DMA

    attended, qkv_own = call(
        attend_own_kernel, (SMEM, VMEM, VMEM), (wide, jax.ShapeDtypeStruct(saved, BF)),
        (pltpu.VMEM((tokens, columns), BF),), "attend_own", **dims,
    )(lengths, block, heads_own)
    first_sum, normed_low, qkv_rest = call(
        attend_rest_kernel, (SMEM, SMEM, VMEM, VMEM, VMEM, VMEM, HBM, HBM),
        (wide, low, jax.ShapeDtypeStruct((others,) + saved, BF)),
        (pltpu.VMEM((others, shard_rows, width), BF), pltpu.VMEM((tokens, columns), BF), dma((others, 8))),
        "attend_rest", **dims,
    )(lengths, offsets, block, attended, first_gain, first_shift, *heads_rest)
    branch, slopes_own = call(
        feed_own_kernel, (VMEM, VMEM, VMEM), (wide, jax.ShapeDtypeStruct((tokens, units), BF)),
        name="feed_own",
    )(normed_low, expand_own, shrink_own)
    feed_scratch = (
        pltpu.VMEM((others, width, units), BF),
        pltpu.VMEM((others, units, width), BF),
        dma((2, others, 8)),
    )
    branch, slopes_rest = call(
        feed_rest_kernel, (SMEM, VMEM, VMEM, HBM, HBM, HBM, HBM),
        (wide, jax.ShapeDtypeStruct((others, tokens, units), BF)), feed_scratch, "feed_rest",
    )(offsets, normed_low, branch, *expand_rest, *shrink_rest)

    member = (
        jnp.arange(inner)[:, None] // bottleneck == jnp.arange(LANES)[None, :]
    ).astype(BF)
    block_spec = pl.BlockSpec((full_len, width), lambda i: (i, 0))
    weight = pl.BlockSpec((width, width), lambda i: (0, 0), pipeline_mode=pl.Buffered(1))
    row = pl.BlockSpec((1, width), lambda i: (0, 0))
    block_output, second_grad, branch_grad, weight_grads, small = pl.pallas_call(
        functools.partial(adapters_kernel, adapters=adapters, scale=width ** (-0.5)),
        grid=(count,),
        in_specs=[
            SMEM, block_spec, block_spec, block_spec, row, row, weight, weight, weight, weight,
            weight, pl.BlockSpec((2, width), lambda i: (0, 0)), row, row,
            pl.BlockSpec((inner, LANES), lambda i: (0, 0)),
        ],
        out_specs=(
            block_spec, block_spec, block_spec,
            pl.BlockSpec((3, width, width), lambda i: (0, 0, 0)),
            pl.BlockSpec((8, width), lambda i: (0, 0)),
        ),
        out_shape=(
            low, wide, low, jax.ShapeDtypeStruct((3, width, width), F32),
            jax.ShapeDtypeStruct((8, width), F32),
        ),
        name="adapters",
    )(
        lengths, branch, first_sum, cotangent, first_gain, first_shift, adapter_down,
        adapter_up.reshape(inner, width), joining_query, joining_key, joining_value, joining_bias,
        final_gain, final_shift, member,
    )

    (normed_grad,) = call(feed_own_back_kernel, (VMEM,) * 5, (wide,), name="feed_own_back")(
        branch_grad, slopes_own, second_grad, expand_own, shrink_own
    )
    first_grad, first_low = call(
        feed_rest_back_kernel, (SMEM, VMEM, VMEM, VMEM, VMEM, VMEM, HBM, HBM, HBM, HBM),
        (wide, low), feed_scratch, "feed_rest_back",
    )(offsets, branch_grad, slopes_rest, normed_grad, first_sum, first_gain, *expand_rest, *shrink_rest)
    grads = (pltpu.VMEM((3, tokens, columns), BF), pltpu.VMEM((tokens, columns), BF))
    (input_grad,) = call(
        attend_own_back_kernel, (SMEM, VMEM, VMEM, VMEM, VMEM), (wide,), grads, "attend_own_back",
        **dims,
    )(lengths, first_low, qkv_own, heads_own, first_grad)
    for r in range(others):
        (input_grad,) = call(
            attend_rest_back_kernel, (SMEM, SMEM, VMEM, VMEM, VMEM, HBM, HBM), (wide,),
            (pltpu.VMEM((1, shard_rows, width), BF),) + grads + (dma((1, 8)),),
            f"attend_rest_back_{r}", others=(r,), **dims,
        )(lengths, offsets, first_low, qkv_rest[r : r + 1], input_grad, *heads_rest)
    return block_output, input_grad, weight_grads, small[:4]


def local(
    block_input,
    lengths,
    head_project,
    head_combine,
    first_gain,
    first_shift,
    expand_weight,
    shrink_weight,
    adapter_down,
    adapter_up,
    joining_query,
    joining_key,
    joining_value,
    joining_bias,
    final_gain,
    final_shift,
    cotangent,
):
    own_count, full_len, width = block_input.shape
    tokens = own_count * full_len
    columns = head_project.shape[2]
    links = Links()
    own_lengths = lax.dynamic_slice_in_dim(lengths, links.mp_index * own_count, own_count)
    heads_own = jnp.concatenate(
        [head_project.transpose(0, 2, 1).reshape(3 * columns, width), head_combine]
    )
    heads_rest = links.gather(heads_own)
    expand_rest = links.gather(expand_weight)
    shrink_rest = links.gather(shrink_weight)
    block_output, input_grad, weight_grads, small = layer(
        own_lengths, block_input.reshape(tokens, width), cotangent.reshape(tokens, width),
        heads_own, expand_weight, shrink_weight, heads_rest, expand_rest, shrink_rest,
        links.offsets(width // 8), first_gain[None], first_shift[None], adapter_down, adapter_up,
        joining_query, joining_key, joining_value, joining_bias, final_gain[None],
        final_shift[None], columns, full_len,
    )
    weight_grads, small = links.total(weight_grads, small)
    return (
        block_output.reshape(block_input.shape),
        input_grad.reshape(block_input.shape),
        weight_grads,
        small[:2],
        small[2],
        small[3],
    )


def solution(mesh):
    return jax.shard_map(
        local,
        mesh=mesh,
        in_specs=(
            P(("dp", "mp"), None, None),
            P("dp"),
            P(None, None, "mp"),
            P("mp", None),
            P(),
            P(),
            P(None, "mp"),
            P("mp", None),
            P(),
            P(),
            P(),
            P(),
            P(),
            P(),
            P(),
            P(),
            P(("dp", "mp"), None, None),
        ),
        out_specs=(P(("dp", "mp"), None, None), P(("dp", "mp"), None, None), P(), P(), P(), P()),
        check_vma=False,
    )
```
